128 devices in a mesh: subj: 8 (over z_lo, y), gz: 16 (over x, z_hi, core).
Axes of the slice: x: 4, y: 4, z: 4 (z_hi: 2, z_lo: 2; z = z_hi * 2 + z_lo), core: 2. Of those that a mesh axis runs over, the one named last changes fastest.
Arguments:
- warped: float32 [8, 512, 64, 256], P('subj', 'gz'), may hold values from -12 to 12
Outputs:
- force: float32 [8, 3, 512, 64, 256], P('subj', None, 'gz')
- template: float32 [512, 64, 256], P('gz')
- loss: float32 [8], P('subj')
The draws below stay inside these ranges and needn't reach their ends.
All inputs are finite; a program needn't handle non-finite values.
Results may differ from the reference program's by a relative error of at most 0.0001.
Values sent between devices are 32-bit elements; how exact they have to be, the bound alone decides.
No kernel may reach another device: no remote copies, remote signals or barrier semaphores. Data moves between devices by JAX's collectives and lax.ppermute only.
A program may use at most 128 MiB of HBM per device.

```python
import math
import jax
import jax.numpy as jnp
from jax import lax

SUBJ = 8
NY = 64
NX = 256
BOX_R = 4
GAUSS_R = 3
NZ = 512


def draw_warped(key, part):
    key_common, key_jitter = jax.random.split(jax.random.fold_in(key, 17))
    heights = jnp.arange(NZ, dtype=jnp.float32) / float(NZ)
    noise_level = (0.3 + 1.7 * heights)[None, :, None, None]
    common = jnp.clip(jax.random.normal(key_common, (1, NZ, NY, NX), jnp.float32), -4.0, 4.0)
    jitter = jnp.clip(jax.random.normal(key_jitter, (SUBJ, NZ, NY, NX), jnp.float32), -4.0, 4.0)
    return (common + noise_level * jitter).astype(jnp.float32)


def setup_inputs(seed: int = 0) -> dict:
    key_of = jax.random.split(jax.random.key(seed), 2)
    return {
        "warped": draw_warped(jax.random.fold_in(key_of[1], 71), 0),
    }


epsilon = 1e-5


def shifted_sum(padded, along, planes_out, window_span):
    running = lax.slice_in_dim(padded, 0, planes_out, axis=along)
    for offset in range(1, window_span):
        running = running + lax.slice_in_dim(padded, offset, offset + planes_out, axis=along)
    return running


def window_mean(volume):
    window_span = 2 * BOX_R + 1
    planes_out = volume.shape[0] - 2 * BOX_R
    running = shifted_sum(volume, 0, planes_out, window_span)
    running = shifted_sum(jnp.pad(running, ((0, 0), (BOX_R, BOX_R), (0, 0))), 1, volume.shape[1], window_span)
    running = shifted_sum(jnp.pad(running, ((0, 0), (0, 0), (BOX_R, BOX_R))), 2, volume.shape[2], window_span)
    return running / float(window_span ** 3)


def local_force(moving, target):
    planes_out = moving.shape[0] - 2 * BOX_R
    mean_moving = window_mean(moving)
    mean_target = window_mean(target)
    var_moving = window_mean(moving * moving) - mean_moving * mean_moving
    var_target = window_mean(target * target) - mean_target * mean_target
    cross_cov = window_mean(moving * target) - mean_moving * mean_target
    moving_core = moving[BOX_R:BOX_R + planes_out]
    target_core = target[BOX_R:BOX_R + planes_out]
    denominator = var_moving * var_target + epsilon
    similarity = cross_cov * cross_cov / denominator
    factor = 2.0 * cross_cov / denominator * ((target_core - mean_target) - cross_cov / (var_moving + epsilon) * (moving_core - mean_moving))
    slope_depth = 0.5 * (moving[BOX_R + 1:BOX_R + 1 + planes_out] - moving[BOX_R - 1:BOX_R - 1 + planes_out])
    padded_rows = jnp.pad(moving_core, ((0, 0), (1, 1), (0, 0)))
    slope_rows = 0.5 * (padded_rows[:, 2:] - padded_rows[:, :-2])
    padded_cols = jnp.pad(moving_core, ((0, 0), (0, 0), (1, 1)))
    slope_cols = 0.5 * (padded_cols[:, :, 2:] - padded_cols[:, :, :-2])
    forces = jnp.stack([factor * slope_depth, factor * slope_rows, factor * slope_cols])
    return forces, similarity


def blur_weights():
    bumps = [math.exp(-(offset * offset) / 8.0) for offset in range(-GAUSS_R, GAUSS_R + 1)]
    whole = sum(bumps)
    return [bump / whole for bump in bumps]


def weighted_sum(padded, along, planes_out, weights):
    running = weights[0] * lax.slice_in_dim(padded, 0, planes_out, axis=along)
    for offset in range(1, len(weights)):
        running = running + weights[offset] * lax.slice_in_dim(padded, offset, offset + planes_out, axis=along)
    return running


def gaussian_blur(padded):
    weights = blur_weights()
    planes_out = padded.shape[1] - 2 * GAUSS_R
    smoothed = weighted_sum(padded, 1, planes_out, weights)
    smoothed = weighted_sum(jnp.pad(smoothed, ((0, 0), (0, 0), (GAUSS_R, GAUSS_R), (0, 0))), 2, padded.shape[2], weights)
    smoothed = weighted_sum(jnp.pad(smoothed, ((0, 0), (0, 0), (0, 0), (GAUSS_R, GAUSS_R))), 3, padded.shape[3], weights)
    return smoothed


def reference(warped):
    template = jnp.sum(warped, axis=0) / SUBJ
    target_wide = jnp.pad(template, ((BOX_R, BOX_R), (0, 0), (0, 0)))
    smoothed_all = []
    losses = []
    for member in range(SUBJ):
        moving_wide = jnp.pad(warped[member], ((BOX_R, BOX_R), (0, 0), (0, 0)))
        forces, similarity = local_force(moving_wide, target_wide)
        padded = jnp.pad(forces, ((0, 0), (GAUSS_R, GAUSS_R), (0, 0), (0, 0)))
        smoothed_all.append(gaussian_blur(padded))
        losses.append(-jnp.sum(similarity) / float(NZ * NY * NX))
    return jnp.stack(smoothed_all), template, jnp.stack(losses)
```

```python
import functools, math
import numpy as np
import jax
import jax.numpy as jnp
from jax import lax
from jax.experimental import pallas as pl
from jax.experimental.pallas import tpu as pltpu

BOX_R = 4
GAUSS_R = 3
epsilon = 1e-05
F32, BF16 = jnp.float32, jnp.bfloat16
H = 7
BZ = 8
INV = 1.0 / 729.0


def blur_weights():
    bumps = [math.exp(-(k * k) / 8.0) for k in range(-GAUSS_R, GAUSS_R + 1)]
    whole = sum(bumps)
    return [b / whole for b in bumps]


def band_ones(nx):
    d = np.abs(np.arange(nx)[:, None] - np.arange(nx)[None, :])
    b = (d <= BOX_R).astype(np.float32)
    return np.concatenate([b, b, b], axis=0)


def split2(m):
    hi = m.astype(jnp.bfloat16).astype(np.float32)
    lo = (m - hi).astype(np.float32)
    return hi, lo


def gauss_x(nx):
    w = np.array(blur_weights(), np.float32)
    d = np.arange(nx)[:, None] - np.arange(nx)[None, :]
    m = np.where(np.abs(d) <= GAUSS_R, w[np.clip(d + GAUSS_R, 0, 2 * GAUSS_R)], 0.0).astype(np.float32)
    hi, lo = split2(m)
    return np.concatenate([hi, hi, lo], axis=0)


def row_of(ny):
    nb = ny // 8
    r = np.arange(ny)
    i, s = r // 8, r % 8
    return s * nb + i


def gauss_y(ny, planes):
    w = np.array(blur_weights(), np.float32)
    y_in = row_of(ny)
    d = y_in[None, :] - np.arange(ny)[:, None]
    m = np.where(np.abs(d) <= GAUSS_R, w[np.clip(d + GAUSS_R, 0, 2 * GAUSS_R)], 0.0).astype(np.float32)
    m = np.kron(np.eye(planes, dtype=np.float32), m)
    hi, lo = split2(m)
    return np.concatenate([hi, hi, lo], axis=1)


def suffix_prefix(first, second):
    n = len(first)
    suf = [None] * n
    suf[n - 1] = first[n - 1]
    for i in range(n - 2, -1, -1):
        suf[i] = first[i] + suf[i + 1]
    out = []
    run = None
    for i in range(n):
        run = second[i] if run is None else run + second[i]
        out.append(suf[i] + run)
    return out


def permute_in(dst, dst_plane, src, src_plane, n, stage):
    def natural(p, c):
        for h in range(2):
            stage[p, h] = src[src_plane + p, :, pl.ds(128 * h, 128)]
        return c
    lax.fori_loop(0, n, natural, 0)

    def body(p, c):
        for i in range(8):
            for h in range(2):
                dst[dst_plane + p, pl.ds(8 * i, 8), pl.ds(128 * h, 128)] = stage[
                    p, h, pl.ds(i, 8, stride=8), :]
        return c
    lax.fori_loop(0, n, body, 0)


def z_sums(out, terms, get_first, get_second):
    def body(q, c):
        rows = pl.ds(pl.multiple_of(q * 8, 8), 8)
        for h in range(2):
            cols = pl.ds(128 * h, 128)
            first = get_first(rows, cols)
            second = get_second(rows, cols)
            for ref, term in zip(out, terms):
                res = suffix_prefix([term(a) for a in first], [term(b) for b in second])
                for p in range(8):
                    ref[p, rows, cols] = res[p]
        return c
    lax.fori_loop(0, 8, body, 0)


def y_sums_split(ref, parts):
    sub = lax.broadcasted_iota(jnp.int32, (8, 128), 0)
    first_row, last_row = sub == 0, sub == 7

    def body(p, c):
        for h in range(2):
            cols = pl.ds(128 * h, 128)
            x = [ref[p, pl.ds(8 * i, 8), cols] for i in range(8)]
            down = [jnp.where(first_row, 0.0, pltpu.roll(x[i], 1, 0)) for i in range(4, 8)]
            up = [jnp.where(last_row, 0.0, pltpu.roll(x[i], 7, 0)) for i in range(4)]
            res = suffix_prefix(down + x[:4], x[4:] + up)
            for j in range(4):
                v = jnp.concatenate([res[2 * j], res[2 * j + 1]], axis=0)
                hi = v.astype(BF16)
                v = v - hi.astype(F32)
                mid = v.astype(BF16)
                lo = (v - mid.astype(F32)).astype(BF16)
                rows = pl.ds(pl.multiple_of(p * 64, 64) + 16 * j, 16)
                parts[rows, pl.ds(128 * h, 128)] = hi
                parts[rows, pl.ds(256 + 128 * h, 128)] = mid
                parts[rows, pl.ds(512 + 128 * h, 128)] = lo
        return c
    lax.fori_loop(0, 8, body, 0)


def x_sums(parts, band, out):
    out[...] = jnp.dot(parts[...], band[...], preferred_element_type=F32).reshape(out.shape)


def fetch_block(k, last, ring, slot, lo, body, hi, stage):
    @pl.when(k == 0)
    def _():
        ring[slot, 0] = jnp.zeros(ring.shape[2:], F32)
        permute_in(ring.at[slot], 1, lo, 0, H, stage)

    @pl.when(jnp.logical_and(k > 0, k < last))
    def _():
        permute_in(ring.at[slot], 0, body, 0, BZ, stage)

    @pl.when(k == last)
    def _():
        permute_in(ring.at[slot], 0, hi, 0, H, stage)
        ring[slot, 7] = jnp.zeros(ring.shape[2:], F32)


def moving_kernel(lo, body, hi, band, ip, mean, var, ring, zs, parts, sums, stage):
    k = pl.program_id(0)
    last = pl.num_programs(0) - 1
    slot = lax.rem(k, 2)
    prev = 1 - slot
    fetch_block(k, last, ring, slot, lo, body, hi, stage)
    ip[...] = ring[slot]

    @pl.when(k > 0)
    def _():
        z_sums(
            [zs.at[0], zs.at[1]],
            [lambda a: a, lambda a: a * a],
            lambda r, c: [ring[prev, p, r, c] for p in range(8)],
            lambda r, c: [ring[slot, p, r, c] for p in range(8)],
        )
        for v in range(2):
            y_sums_split(zs.at[v], parts)
            x_sums(parts, band, sums.at[v])

        def point(p, c):
            m = sums[0, p] * INV
            mean[p] = m
            var[p] = sums[1, p] * INV - m * m
            return c
        lax.fori_loop(0, 8, point, 0)


def blk(f):
    return pl.BlockSpec((BZ, 64, 256), f)


def whole(shape):
    return pl.BlockSpec(shape, lambda k: (0,) * len(shape))


def params(**kw):
    return pltpu.CompilerParams(vmem_limit_bytes=60 * 1024 * 1024, **kw)


def moving_call(moving, lo, hi):
    n = moving.shape[0] // BZ
    plane = moving.shape[1:]
    band = jnp.asarray(band_ones(256), BF16)
    clip = lambda k: jnp.clip(k - 1, 0, n - 1)
    return pl.pallas_call(
        moving_kernel,
        name="moving",
        grid=(n + 2,),
        in_specs=[whole(lo.shape), blk(lambda k: (clip(k), 0, 0)), whole(hi.shape), whole(band.shape)],
        out_specs=[blk(lambda k: (k, 0, 0)), blk(lambda k: (jnp.maximum(k - 1, 0), 0, 0)), blk(lambda k: (jnp.maximum(k - 1, 0), 0, 0))],
        out_shape=[jax.ShapeDtypeStruct(((n + 2) * BZ,) + plane, F32)] + [jax.ShapeDtypeStruct(((n + 1) * BZ,) + plane, F32)] * 2,
        scratch_shapes=[
            pltpu.VMEM((2, BZ, 64, 256), F32),
            pltpu.VMEM((2, BZ, 64, 256), F32),
            pltpu.VMEM((BZ * 64, 768), BF16),
            pltpu.VMEM((2, BZ, 64, 256), F32),
            pltpu.VMEM((BZ, 2, 64, 128), F32),
        ],
        compiler_params=params(),
    )(lo, moving, hi, band)


def factor_kernel(edge, lo, body, hi, ia, ib, mean, var, band, fac, loss, ring, zs, parts, sums, stage):
    k = pl.program_id(0)
    last = pl.num_programs(0) - 1
    slot = lax.rem(k, 2)
    prev = 1 - slot
    fetch_block(k, last, ring, slot, lo, body, hi, stage)

    @pl.when(k == 0)
    def _():
        loss[...] = jnp.zeros(loss.shape, F32)

    @pl.when(k > 0)
    def _():
        z_sums(
            [zs.at[0], zs.at[1]],
            [lambda a: a, lambda a: a * a],
            lambda r, c: [ring[prev, p, r, c] for p in range(8)],
            lambda r, c: [ring[slot, p, r, c] for p in range(8)],
        )
        z_sums(
            [zs.at[2]],
            [lambda a: a[0] * a[1]],
            lambda r, c: [(ring[prev, p, r, c], ia[p, r, c]) for p in range(8)],
            lambda r, c: [(ring[slot, p, r, c], ib[p, r, c]) for p in range(8)],
        )
        for v in range(3):
            y_sums_split(zs.at[v], parts)
            x_sums(parts, band, sums.at[v])

        def point(t, c):
            p = t >> 2
            rows = pl.ds(pl.multiple_of(lax.rem(t, 4) * 16, 16), 16)
            plane = (k - 1) * BZ - 4 + p
            inside = jnp.logical_and(plane >= 0, plane < (last - 1) * BZ)
            keep = jnp.logical_or(inside, jnp.where(plane < 0, edge[0], edge[1]) == 0)
            src_slot = jnp.where(p < 4, prev, slot)
            q = jnp.where(p < 4, p + 4, p - 4)
            j0 = ring[src_slot, q, rows, :]
            i0 = jnp.where(p < 4, ia[q, rows, :], ib[q, rows, :])
            mj = sums[0, p, rows, :] * INV
            vj = sums[1, p, rows, :] * INV - mj * mj
            mi = mean[p, rows, :]
            vi = var[p, rows, :]
            cc = sums[2, p, rows, :] * INV - mi * mj
            d1 = vi * vj + epsilon
            e = cc / d1
            sim = cc * e
            f = e * ((j0 - mj) - cc / (vi + epsilon) * (i0 - mi))
            fac[p, rows, :] = jnp.where(keep, f, 0.0)
            loss[...] += jnp.where(inside, sim, 0.0)
            return c
        lax.fori_loop(0, 32, point, 0)


def factor_call(edge, template, lo, hi, ip, mean, var):
    n = template.shape[0] // BZ
    plane = template.shape[1:]
    band = jnp.asarray(band_ones(256), BF16)
    clip = lambda k: jnp.clip(k - 1, 0, n - 1)
    back = lambda k: jnp.maximum(k - 1, 0)
    return pl.pallas_call(
        factor_kernel,
        name="factor",
        grid=(n + 2,),
        in_specs=[
            pl.BlockSpec(memory_space=pltpu.SMEM),
            whole(lo.shape), blk(lambda k: (clip(k), 0, 0)), whole(hi.shape),
            blk(lambda k: (back(k), 0, 0)), blk(lambda k: (jnp.maximum(k, 1), 0, 0)),
            blk(lambda k: (back(k), 0, 0)), blk(lambda k: (back(k), 0, 0)),
            whole(band.shape),
        ],
        out_specs=[blk(lambda k: (back(k), 0, 0)), whole((16, 256))],
        out_shape=[jax.ShapeDtypeStruct(((n + 1) * BZ,) + plane, F32), jax.ShapeDtypeStruct((16, 256), F32)],
        scratch_shapes=[
            pltpu.VMEM((2, BZ, 64, 256), F32),
            pltpu.VMEM((3, BZ, 64, 256), F32),
            pltpu.VMEM((BZ * 64, 768), BF16),
            pltpu.VMEM((3, BZ, 64, 256), F32),
            pltpu.VMEM((BZ, 2, 64, 128), F32),
        ],
        compiler_params=params(),
    )(edge, lo, template, hi, ip, ip, mean, var, band)


def smooth_kernel(fac, ia, ib, ax, ay, out, ring, xp, xs, yp):
    k = pl.program_id(0)
    slot = lax.rem(k, 2)
    prev = 1 - slot
    sub = lax.broadcasted_iota(jnp.int32, (8, 128), 0)
    lane = lax.broadcasted_iota(jnp.int32, (8, 128), 1)

    def raw(p, q, mid, before, after):
        f = [[fac[p, pl.ds(8 * i, 8), pl.ds(128 * h, 128)] for h in range(2)] for i in range(8)]
        im = [[mid[q, pl.ds(8 * i, 8), pl.ds(128 * h, 128)] for h in range(2)] for i in range(8)]
        for i in range(8):
            rows = pl.ds(8 * i, 8)
            for h in range(2):
                cols = pl.ds(128 * h, 128)
                ring[slot, 0, p, rows, cols] = f[i][h] * (after(rows, cols) - before(rows, cols))
                up = im[i + 1][h] if i < 7 else jnp.where(sub == 7, 0.0, pltpu.roll(im[0][h], 7, 0))
                dn = im[i - 1][h] if i > 0 else jnp.where(sub == 0, 0.0, pltpu.roll(im[7][h], 1, 0))
                ring[slot, 1, p, rows, cols] = f[i][h] * (up - dn)
            left = [pltpu.roll(im[i][h], 127, 1) for h in range(2)]
            right = [pltpu.roll(im[i][h], 1, 1) for h in range(2)]
            e, s = lane == 127, lane == 0
            nxt = [jnp.where(e, left[1], left[0]), jnp.where(e, 0.0, left[1])]
            prv = [jnp.where(s, 0.0, right[0]), jnp.where(s, right[0], right[1])]
            for h in range(2):
                ring[slot, 2, p, rows, pl.ds(128 * h, 128)] = f[i][h] * (nxt[h] - prv[h])

    def lower(p, c):
        raw(p, p + 4, ia, lambda r, cc: ia[p + 3, r, cc], lambda r, cc: ia[p + 5, r, cc])
        return c

    def upper(p, c):
        raw(p, p - 4, ib, lambda r, cc: ib[p - 5, r, cc], lambda r, cc: ib[p - 3, r, cc])
        return c
    lax.fori_loop(0, 3, lower, 0)
    raw(3, 7, ia, lambda r, cc: ia[6, r, cc], lambda r, cc: ib[0, r, cc])
    raw(4, 0, ib, lambda r, cc: ia[7, r, cc], lambda r, cc: ib[1, r, cc])
    lax.fori_loop(5, 8, upper, 0)

    w = [float(v) for v in blur_weights()]

    @pl.when(k > 0)
    def _():
        for comp in range(3):
            def z_pass(q, c):
                rows = pl.ds(pl.multiple_of(q * 16, 16), 16)
                for h in range(2):
                    cols = pl.ds(128 * h, 128)
                    x = [ring[prev, comp, p, rows, cols] for p in range(1, 8)] + [
                        ring[slot, comp, p, rows, cols] for p in range(0, 7)]
                    for p in range(8):
                        v = w[3] * x[p + 3]
                        for d in range(1, 4):
                            v = v + w[3 - d] * (x[p + 3 - d] + x[p + 3 + d])
                        hi = v.astype(BF16)
                        lo = (v - hi.astype(F32)).astype(BF16)
                        dst = pl.ds(64 * p + pl.multiple_of(q * 16, 16), 16)
                        xp[dst, pl.ds(128 * h, 128)] = hi
                        xp[dst, pl.ds(256 + 128 * h, 128)] = lo
                        xp[dst, pl.ds(512 + 128 * h, 128)] = hi
                return c
            lax.fori_loop(0, 4, z_pass, 0)
            xs[...] = jnp.dot(xp[...], ax[...], preferred_element_type=F32)

            def split(t, c):
                rows = pl.ds(pl.multiple_of(t * 32, 32), 32)
                v = xs[rows, :]
                hi = v.astype(BF16)
                g = t >> 3
                r = pl.multiple_of(lax.rem(t, 8) * 32, 32)
                yp[g, pl.ds(r, 32), :] = hi
                yp[g, pl.ds(256 + r, 32), :] = (v - hi.astype(F32)).astype(BF16)
                yp[g, pl.ds(512 + r, 32), :] = hi
                return c
            lax.fori_loop(0, 16, split, 0)
            for g in range(2):
                out[comp, pl.ds(4 * g, 4)] = jnp.dot(
                    ay[...], yp[g], preferred_element_type=F32).reshape(4, 64, 256)


def smooth_call(fac, ip):
    n = fac.shape[0] // BZ - 1
    plane = fac.shape[1:]
    ax = jnp.asarray(gauss_x(256), BF16)
    ay = jnp.asarray(gauss_y(64, 4), BF16)
    return pl.pallas_call(
        smooth_kernel,
        name="smooth",
        grid=(n + 1,),
        in_specs=[blk(lambda k: (k, 0, 0)), blk(lambda k: (k, 0, 0)), blk(lambda k: (k + 1, 0, 0)),
                  whole(ax.shape), whole(ay.shape)],
        out_specs=pl.BlockSpec((3, BZ, 64, 256), lambda k: (0, jnp.maximum(k - 1, 0), 0, 0)),
        out_shape=jax.ShapeDtypeStruct((3, n * BZ) + plane, F32),
        scratch_shapes=[
            pltpu.VMEM((2, 3, BZ, 64, 256), F32),
            pltpu.VMEM((BZ * 64, 768), BF16),
            pltpu.VMEM((BZ * 64, 256), F32),
            pltpu.VMEM((2, 768, 256), BF16),
        ],
        compiler_params=params(),
    )(fac, ip, ip, ax, ay)


from jax.sharding import PartitionSpec as P


def halos(array, axis, width):
    size = lax.axis_size(axis)
    up = [(i, i + 1) for i in range(size - 1)]
    down = [(j, i) for i, j in up]
    lo = lax.ppermute(array[-width:], axis, up)
    hi = lax.ppermute(array[:width], axis, down)
    return lo, hi


def on_device(warped):
    moving = warped[0]
    planes = moving.shape[0]
    g, size = lax.axis_index("gz"), lax.axis_size("gz")
    edge = jnp.stack([g == 0, g == size - 1]).astype(jnp.int32)
    lo, hi = halos(moving, "gz", H)
    template = lax.psum(moving, "subj") / lax.axis_size("subj")
    ip, mean, var = moving_call(moving, lo, hi)
    tlo, thi = halos(template, "gz", H)
    fac, part = factor_call(edge, template, tlo, thi, ip, mean, var)
    cells = float(size * planes * moving.shape[1] * moving.shape[2])
    loss = -lax.psum(jnp.sum(part), "gz") / cells
    force = smooth_call(fac, ip)
    return force[None], template, jnp.reshape(loss, (1,))


def solution(mesh):
    return jax.shard_map(
        on_device,
        mesh=mesh,
        in_specs=(P("subj", "gz", None, None),),
        out_specs=(P("subj", None, "gz", None, None), P("gz", None, None), P("subj")),
        check_vma=False,
    )
```

```python
import functools, math
import numpy as np
import jax
import jax.numpy as jnp
from jax import lax
from jax.experimental import pallas as pl
from jax.experimental.pallas import tpu as pltpu

BOX_R = 4
GAUSS_R = 3
epsilon = 1e-05
F32, BF16 = jnp.float32, jnp.bfloat16
BZ = 8
INV = 1.0 / 729.0


def blur_weights():
    bumps = [math.exp(-(k * k) / 8.0) for k in range(-GAUSS_R, GAUSS_R + 1)]
    whole = sum(bumps)
    return [b / whole for b in bumps]


def band_ones(nx):
    d = np.abs(np.arange(nx)[:, None] - np.arange(nx)[None, :])
    b = (d <= BOX_R).astype(np.float32)
    return np.concatenate([b, b, b], axis=0)


def split2(m):
    hi = m.astype(jnp.bfloat16).astype(np.float32)
    lo = (m - hi).astype(np.float32)
    return hi, lo


def gauss_x(nx):
    w = np.array(blur_weights(), np.float32)
    d = np.arange(nx)[:, None] - np.arange(nx)[None, :]
    m = np.where(np.abs(d) <= GAUSS_R, w[np.clip(d + GAUSS_R, 0, 2 * GAUSS_R)], 0.0).astype(np.float32)
    hi, lo = split2(m)
    return np.concatenate([hi, hi, lo], axis=0)


def row_of(ny):
    nb = ny // 8
    r = np.arange(ny)
    i, s = r // 8, r % 8
    return s * nb + i


def gauss_y(ny, planes):
    w = np.array(blur_weights(), np.float32)
    y_in = row_of(ny)
    d = y_in[None, :] - np.arange(ny)[:, None]
    m = np.where(np.abs(d) <= GAUSS_R, w[np.clip(d + GAUSS_R, 0, 2 * GAUSS_R)], 0.0).astype(np.float32)
    m = np.kron(np.eye(planes, dtype=np.float32), m)
    hi, lo = split2(m)
    return np.concatenate([hi, hi, lo], axis=1)


def suffix_prefix(first, second):
    n = len(first)
    suf = [None] * n
    suf[n - 1] = first[n - 1]
    for i in range(n - 2, -1, -1):
        suf[i] = first[i] + suf[i + 1]
    out = []
    run = None
    for i in range(n):
        run = second[i] if run is None else run + second[i]
        out.append(suf[i] + run)
    return out


PEERS = ((0, 0), (1, 2), (0, 2), (1, 1), (1, 3), (0, 1), (0, 3), (1, 0))


def peer(s, dz, dy):
    return (s & 4) ^ (4 * dz) | ((s + dy) & 3)


def pack_kernel(me, src, full, head, tail, *rest):
    pieces, stage = rest[:-1], rest[-1]
    k = pl.program_id(0)
    idx = [peer(me[0], dz, dy) for dz, dy in PEERS]

    def natural(p, c):
        for h in range(2):
            stage[p, h] = src[p, :, pl.ds(128 * h, 128)]
        return c
    lax.fori_loop(0, BZ, natural, 0)

    def body(p, c):
        for h in range(2):
            for i in range(8):
                full[p, pl.ds(8 * i, 8), pl.ds(128 * h, 128)] = stage[p, h, pl.ds(i, 8, stride=8), :]
            for j, ref in enumerate(pieces):
                ref[p, :, pl.ds(128 * h, 128)] = stage[p, h, pl.ds(idx[j], 8, stride=8), :]
        return c
    lax.fori_loop(0, BZ, body, 0)

    @pl.when(k == 0)
    def _():
        head[...] = full[...]

    @pl.when(k == pl.num_programs(0) - 1)
    def _():
        tail[...] = full[...]


def pack_call(me, moving):
    planes = moving.shape[0]
    n = planes // BZ
    plane = moving.shape[1:]
    members = len(PEERS)
    block = jax.ShapeDtypeStruct((BZ,) + plane, F32)
    return pl.pallas_call(
        pack_kernel,
        name="pack",
        grid=(n,),
        in_specs=[pl.BlockSpec(memory_space=pltpu.SMEM), blk(lambda k: (k, 0, 0))],
        out_specs=[blk(lambda k: (k, 0, 0)), whole(block.shape), whole(block.shape)]
        + [pl.BlockSpec((BZ, 8, 256), lambda k: (k, 0, 0))] * members,
        out_shape=[jax.ShapeDtypeStruct(moving.shape, F32), block, block]
        + [jax.ShapeDtypeStruct((planes, 8, 256), F32)] * members,
        scratch_shapes=[pltpu.VMEM((BZ, 2, 64, 128), F32)],
        compiler_params=params(),
    )(me, moving)


def gather_kernel(me, *refs):
    n = len(refs) - 2
    idx = [peer(me[0], dz, dy) for dz, dy in PEERS]
    pieces, full, sem = refs[:n], refs[n], refs[n + 1]
    copies = []
    for j in range(n):
        rows = pl.ds(pl.multiple_of(idx[j] * 8, 8), 8)
        copies.append(pltpu.make_async_copy(pieces[j], full.at[:, rows, :], sem.at[j]))
        copies[-1].start()
    for copy in copies:
        copy.wait()


def gather_call(me, pieces):
    n = len(pieces)
    planes, _, nx = pieces[0].shape
    return pl.pallas_call(
        gather_kernel,
        name="gather",
        in_specs=[pl.BlockSpec(memory_space=pltpu.SMEM)] + [pl.BlockSpec(memory_space=pl.ANY)] * n,
        out_specs=pl.BlockSpec(memory_space=pl.ANY),
        out_shape=jax.ShapeDtypeStruct((planes, 8 * n, nx), F32),
        scratch_shapes=[pltpu.SemaphoreType.DMA((n,))],
        compiler_params=params(),
    )(me, *pieces)


def natural_kernel(src, dst, stage):
    def rows(p, c):
        for h in range(2):
            stage[p, h] = src[p, :, pl.ds(128 * h, 128)]
        return c
    lax.fori_loop(0, BZ, rows, 0)

    def body(p, c):
        for h in range(2):
            for i in range(8):
                dst[p, pl.ds(8 * i, 8), pl.ds(128 * h, 128)] = stage[p, h, pl.ds(i, 8, stride=8), :]
        return c
    lax.fori_loop(0, BZ, body, 0)


def natural_call(array):
    return pl.pallas_call(
        natural_kernel,
        name="natural",
        grid=(array.shape[0] // BZ,),
        in_specs=[blk(lambda k: (k, 0, 0))],
        out_specs=blk(lambda k: (k, 0, 0)),
        out_shape=jax.ShapeDtypeStruct(array.shape, F32),
        scratch_shapes=[pltpu.VMEM((BZ, 2, 64, 128), F32)],
        compiler_params=params(),
    )(array)


def z_sums(out, terms, get_first, get_second):
    def body(q, c):
        rows = pl.ds(pl.multiple_of(q * 8, 8), 8)
        for h in range(2):
            cols = pl.ds(128 * h, 128)
            first = get_first(rows, cols)
            second = get_second(rows, cols)
            for ref, term in zip(out, terms):
                res = suffix_prefix([term(a) for a in first], [term(b) for b in second])
                for p in range(8):
                    ref[p, rows, cols] = res[p]
        return c
    lax.fori_loop(0, 8, body, 0)


def y_sums_split(ref, parts):
    sub = lax.broadcasted_iota(jnp.int32, (8, 128), 0)
    first_row, last_row = sub == 0, sub == 7

    def body(p, c):
        for h in range(2):
            cols = pl.ds(128 * h, 128)
            x = [ref[p, pl.ds(8 * i, 8), cols] for i in range(8)]
            down = [jnp.where(first_row, 0.0, pltpu.roll(x[i], 1, 0)) for i in range(4, 8)]
            up = [jnp.where(last_row, 0.0, pltpu.roll(x[i], 7, 0)) for i in range(4)]
            res = suffix_prefix(down + x[:4], x[4:] + up)
            for j in range(4):
                v = jnp.concatenate([res[2 * j], res[2 * j + 1]], axis=0)
                hi = v.astype(BF16)
                v = v - hi.astype(F32)
                mid = v.astype(BF16)
                lo = (v - mid.astype(F32)).astype(BF16)
                rows = pl.ds(pl.multiple_of(p * 64, 64) + 16 * j, 16)
                parts[rows, pl.ds(128 * h, 128)] = hi
                parts[rows, pl.ds(256 + 128 * h, 128)] = mid
                parts[rows, pl.ds(512 + 128 * h, 128)] = lo
        return c
    lax.fori_loop(0, 8, body, 0)


def x_sums(parts, band, out):
    out[...] = jnp.dot(parts[...], band[...], preferred_element_type=F32).reshape(out.shape)


def fetch_block(k, last, ring, slot, lo, body, hi):
    @pl.when(k == 0)
    def _():
        ring[slot] = lo[...]

    @pl.when(jnp.logical_and(k > 0, k < last))
    def _():
        ring[slot] = body[...]

    @pl.when(k == last)
    def _():
        ring[slot] = hi[...]


def moving_kernel(lo, body, hi, band, ip, mean, var, ring, zs, parts, sums):
    k = pl.program_id(0)
    last = pl.num_programs(0) - 1
    slot = lax.rem(k, 2)
    prev = 1 - slot
    fetch_block(k, last, ring, slot, lo, body, hi)
    ip[...] = ring[slot]

    @pl.when(k > 0)
    def _():
        z_sums(
            [zs.at[0], zs.at[1]],
            [lambda a: a, lambda a: a * a],
            lambda r, c: [ring[prev, p, r, c] for p in range(8)],
            lambda r, c: [ring[slot, p, r, c] for p in range(8)],
        )
        for v in range(2):
            y_sums_split(zs.at[v], parts)
            x_sums(parts, band, sums.at[v])

        def point(p, c):
            m = sums[0, p] * INV
            mean[p] = m
            var[p] = sums[1, p] * INV - m * m
            return c
        lax.fori_loop(0, 8, point, 0)


def blk(f):
    return pl.BlockSpec((BZ, 64, 256), f)


def whole(shape):
    return pl.BlockSpec(shape, lambda k: (0,) * len(shape))


def params(**kw):
    return pltpu.CompilerParams(vmem_limit_bytes=60 * 1024 * 1024, **kw)


def moving_call(moving, lo, hi):
    n = moving.shape[0] // BZ
    plane = moving.shape[1:]
    band = jnp.asarray(band_ones(256), BF16)
    clip = lambda k: jnp.clip(k - 1, 0, n - 1)
    return pl.pallas_call(
        moving_kernel,
        name="moving",
        grid=(n + 2,),
        in_specs=[whole(lo.shape), blk(lambda k: (clip(k), 0, 0)), whole(hi.shape), whole(band.shape)],
        out_specs=[blk(lambda k: (k, 0, 0)), blk(lambda k: (jnp.maximum(k - 1, 0), 0, 0)), blk(lambda k: (jnp.maximum(k - 1, 0), 0, 0))],
        out_shape=[jax.ShapeDtypeStruct(((n + 2) * BZ,) + plane, F32)] + [jax.ShapeDtypeStruct(((n + 1) * BZ,) + plane, F32)] * 2,
        scratch_shapes=[
            pltpu.VMEM((2, BZ, 64, 256), F32),
            pltpu.VMEM((2, BZ, 64, 256), F32),
            pltpu.VMEM((BZ * 64, 768), BF16),
            pltpu.VMEM((2, BZ, 64, 256), F32),
        ],
        compiler_params=params(),
    )(lo, moving, hi, band)


def factor_kernel(edge, lo, body, hi, ia, ib, mean, var, band, fac, loss, ring, zs, parts, sums):
    k = pl.program_id(0)
    last = pl.num_programs(0) - 1
    slot = lax.rem(k, 2)
    prev = 1 - slot
    fetch_block(k, last, ring, slot, lo, body, hi)

    @pl.when(k == 0)
    def _():
        loss[...] = jnp.zeros(loss.shape, F32)

    @pl.when(k > 0)
    def _():
        z_sums(
            [zs.at[0], zs.at[1]],
            [lambda a: a, lambda a: a * a],
            lambda r, c: [ring[prev, p, r, c] for p in range(8)],
            lambda r, c: [ring[slot, p, r, c] for p in range(8)],
        )
        z_sums(
            [zs.at[2]],
            [lambda a: a[0] * a[1]],
            lambda r, c: [(ring[prev, p, r, c], ia[p, r, c]) for p in range(8)],
            lambda r, c: [(ring[slot, p, r, c], ib[p, r, c]) for p in range(8)],
        )
        for v in range(3):
            y_sums_split(zs.at[v], parts)
            x_sums(parts, band, sums.at[v])

        def point(t, c):
            p = t >> 2
            rows = pl.ds(pl.multiple_of(lax.rem(t, 4) * 16, 16), 16)
            plane = (k - 1) * BZ - 4 + p
            inside = jnp.logical_and(plane >= 0, plane < (last - 1) * BZ)
            keep = jnp.logical_or(inside, jnp.where(plane < 0, edge[0], edge[1]) == 0)
            src_slot = jnp.where(p < 4, prev, slot)
            q = jnp.where(p < 4, p + 4, p - 4)
            j0 = ring[src_slot, q, rows, :]
            i0 = jnp.where(p < 4, ia[q, rows, :], ib[q, rows, :])
            mj = sums[0, p, rows, :] * INV
            vj = sums[1, p, rows, :] * INV - mj * mj
            mi = mean[p, rows, :]
            vi = var[p, rows, :]
            cc = sums[2, p, rows, :] * INV - mi * mj
            d1 = vi * vj + epsilon
            e = cc / d1
            sim = cc * e
            f = e * ((j0 - mj) - cc / (vi + epsilon) * (i0 - mi))
            fac[p, rows, :] = jnp.where(keep, f, 0.0)
            loss[...] += jnp.where(inside, sim, 0.0)
            return c
        lax.fori_loop(0, 32, point, 0)


def factor_call(edge, template, lo, hi, ip, mean, var):
    n = template.shape[0] // BZ
    plane = template.shape[1:]
    band = jnp.asarray(band_ones(256), BF16)
    clip = lambda k: jnp.clip(k - 1, 0, n - 1)
    back = lambda k: jnp.maximum(k - 1, 0)
    return pl.pallas_call(
        factor_kernel,
        name="factor",
        grid=(n + 2,),
        in_specs=[
            pl.BlockSpec(memory_space=pltpu.SMEM),
            whole(lo.shape), blk(lambda k: (clip(k), 0, 0)), whole(hi.shape),
            blk(lambda k: (back(k), 0, 0)), blk(lambda k: (jnp.maximum(k, 1), 0, 0)),
            blk(lambda k: (back(k), 0, 0)), blk(lambda k: (back(k), 0, 0)),
            whole(band.shape),
        ],
        out_specs=[blk(lambda k: (back(k), 0, 0)), whole((16, 256))],
        out_shape=[jax.ShapeDtypeStruct(((n + 1) * BZ,) + plane, F32), jax.ShapeDtypeStruct((16, 256), F32)],
        scratch_shapes=[
            pltpu.VMEM((2, BZ, 64, 256), F32),
            pltpu.VMEM((3, BZ, 64, 256), F32),
            pltpu.VMEM((BZ * 64, 768), BF16),
            pltpu.VMEM((3, BZ, 64, 256), F32),
        ],
        compiler_params=params(),
    )(edge, lo, template, hi, ip, ip, mean, var, band)


def smooth_kernel(fac, ia, ib, ax, ay, out, ring, xp, xs, yp):
    k = pl.program_id(0)
    slot = lax.rem(k, 2)
    prev = 1 - slot
    sub = lax.broadcasted_iota(jnp.int32, (8, 128), 0)
    lane = lax.broadcasted_iota(jnp.int32, (8, 128), 1)

    def raw(p, q, mid, before, after):
        f = [[fac[p, pl.ds(8 * i, 8), pl.ds(128 * h, 128)] for h in range(2)] for i in range(8)]
        im = [[mid[q, pl.ds(8 * i, 8), pl.ds(128 * h, 128)] for h in range(2)] for i in range(8)]
        for i in range(8):
            rows = pl.ds(8 * i, 8)
            for h in range(2):
                cols = pl.ds(128 * h, 128)
                ring[slot, 0, p, rows, cols] = f[i][h] * (after(rows, cols) - before(rows, cols))
                up = im[i + 1][h] if i < 7 else jnp.where(sub == 7, 0.0, pltpu.roll(im[0][h], 7, 0))
                dn = im[i - 1][h] if i > 0 else jnp.where(sub == 0, 0.0, pltpu.roll(im[7][h], 1, 0))
                ring[slot, 1, p, rows, cols] = f[i][h] * (up - dn)
            left = [pltpu.roll(im[i][h], 127, 1) for h in range(2)]
            right = [pltpu.roll(im[i][h], 1, 1) for h in range(2)]
            e, s = lane == 127, lane == 0
            nxt = [jnp.where(e, left[1], left[0]), jnp.where(e, 0.0, left[1])]
            prv = [jnp.where(s, 0.0, right[0]), jnp.where(s, right[0], right[1])]
            for h in range(2):
                ring[slot, 2, p, rows, pl.ds(128 * h, 128)] = f[i][h] * (nxt[h] - prv[h])

    def lower(p, c):
        raw(p, p + 4, ia, lambda r, cc: ia[p + 3, r, cc], lambda r, cc: ia[p + 5, r, cc])
        return c

    def upper(p, c):
        raw(p, p - 4, ib, lambda r, cc: ib[p - 5, r, cc], lambda r, cc: ib[p - 3, r, cc])
        return c
    lax.fori_loop(0, 3, lower, 0)
    raw(3, 7, ia, lambda r, cc: ia[6, r, cc], lambda r, cc: ib[0, r, cc])
    raw(4, 0, ib, lambda r, cc: ia[7, r, cc], lambda r, cc: ib[1, r, cc])
    lax.fori_loop(5, 8, upper, 0)

    w = [float(v) for v in blur_weights()]

    @pl.when(k > 0)
    def _():
        for comp in range(3):
            def z_pass(q, c):
                rows = pl.ds(pl.multiple_of(q * 16, 16), 16)
                for h in range(2):
                    cols = pl.ds(128 * h, 128)
                    x = [ring[prev, comp, p, rows, cols] for p in range(1, 8)] + [
                        ring[slot, comp, p, rows, cols] for p in range(0, 7)]
                    for p in range(8):
                        v = w[3] * x[p + 3]
                        for d in range(1, 4):
                            v = v + w[3 - d] * (x[p + 3 - d] + x[p + 3 + d])
                        hi = v.astype(BF16)
                        lo = (v - hi.astype(F32)).astype(BF16)
                        dst = pl.ds(64 * p + pl.multiple_of(q * 16, 16), 16)
                        xp[dst, pl.ds(128 * h, 128)] = hi
                        xp[dst, pl.ds(256 + 128 * h, 128)] = lo
                        xp[dst, pl.ds(512 + 128 * h, 128)] = hi
                return c
            lax.fori_loop(0, 4, z_pass, 0)
            xs[...] = jnp.dot(xp[...], ax[...], preferred_element_type=F32)

            def split(t, c):
                rows = pl.ds(pl.multiple_of(t * 32, 32), 32)
                v = xs[rows, :]
                hi = v.astype(BF16)
                g = t >> 3
                r = pl.multiple_of(lax.rem(t, 8) * 32, 32)
                yp[g, pl.ds(r, 32), :] = hi
                yp[g, pl.ds(256 + r, 32), :] = (v - hi.astype(F32)).astype(BF16)
                yp[g, pl.ds(512 + r, 32), :] = hi
                return c
            lax.fori_loop(0, 16, split, 0)
            for g in range(2):
                out[comp, pl.ds(4 * g, 4)] = jnp.dot(
                    ay[...], yp[g], preferred_element_type=F32).reshape(4, 64, 256)


def smooth_call(fac, ip):
    n = fac.shape[0] // BZ - 1
    plane = fac.shape[1:]
    ax = jnp.asarray(gauss_x(256), BF16)
    ay = jnp.asarray(gauss_y(64, 4), BF16)
    return pl.pallas_call(
        smooth_kernel,
        name="smooth",
        grid=(n + 1,),
        in_specs=[blk(lambda k: (k, 0, 0)), blk(lambda k: (k, 0, 0)), blk(lambda k: (k + 1, 0, 0)),
                  whole(ax.shape), whole(ay.shape)],
        out_specs=pl.BlockSpec((3, BZ, 64, 256), lambda k: (0, jnp.maximum(k - 1, 0), 0, 0)),
        out_shape=jax.ShapeDtypeStruct((3, n * BZ) + plane, F32),
        scratch_shapes=[
            pltpu.VMEM((2, 3, BZ, 64, 256), F32),
            pltpu.VMEM((BZ * 64, 768), BF16),
            pltpu.VMEM((BZ * 64, 256), F32),
            pltpu.VMEM((2, 768, 256), BF16),
        ],
        compiler_params=params(),
    )(fac, ip, ip, ax, ay)


from jax.sharding import PartitionSpec as P


def shift(array, axis, step):
    size = lax.axis_size(axis)
    return lax.ppermute(array, axis, [(i, i + step) for i in range(size) if 0 <= i + step < size])


def on_device(warped):
    moving = warped[0]
    planes = moving.shape[0]
    g, size = lax.axis_index("gz"), lax.axis_size("gz")
    edge = jnp.stack([g == 0, g == size - 1]).astype(jnp.int32)
    me = jnp.reshape(lax.axis_index("subj"), (1,)).astype(jnp.int32)
    pairs = [[(i, peer(i, dz, dy)) for i in range(8)] for dz, dy in PEERS]
    back = [[(b, a) for a, b in pair] for pair in pairs]

    full, head, tail, *pieces = pack_call(me, moving)
    got = [lax.ppermute(piece, "subj", pair) for piece, pair in zip(pieces[1:], pairs[1:])]
    lo, hi = shift(tail, "gz", 1), shift(head, "gz", -1)
    ip, mean, var = moving_call(full, lo, hi)
    got, mean, var = lax.optimization_barrier((got, mean, var))
    own = pieces[0]
    for piece in got:
        own = own + piece
    own = own * 0.125
    got = [own] + [lax.ppermute(own, "subj", pair) for pair in back[1:]]
    target = gather_call(me, got)
    tlo, thi = shift(target[-BZ:], "gz", 1), shift(target[:BZ], "gz", -1)
    fac, part = factor_call(edge, target, tlo, thi, ip, mean, var)
    total = jnp.sum(part)
    step = 1
    while step < size:
        total = total + lax.ppermute(total, "gz", [(i, i ^ step) for i in range(size)])
        step *= 2
    cells = float(size * planes * moving.shape[1] * moving.shape[2])
    loss = -total / cells
    force = smooth_call(fac, ip)
    return force[None], natural_call(target), jnp.reshape(loss, (1,))


def solution(mesh):
    return jax.shard_map(
        on_device,
        mesh=mesh,
        in_specs=(P("subj", "gz", None, None),),
        out_specs=(P("subj", None, "gz", None, None), P("gz", None, None), P("subj")),
        check_vma=False,
    )
```

```python
import functools, math
import numpy as np
import jax
import jax.numpy as jnp
from jax import lax
from jax.experimental import pallas as pl
from jax.experimental.pallas import tpu as pltpu

BOX_R = 4
GAUSS_R = 3
epsilon = 1e-05
F32, BF16 = jnp.float32, jnp.bfloat16
BZ = 8
INV = 1.0 / 729.0


def blur_weights():
    bumps = [math.exp(-(k * k) / 8.0) for k in range(-GAUSS_R, GAUSS_R + 1)]
    whole = sum(bumps)
    return [b / whole for b in bumps]


def band_ones(nx):
    d = np.abs(np.arange(nx)[:, None] - np.arange(nx)[None, :])
    b = (d <= BOX_R).astype(np.float32)
    return np.concatenate([b, b, b], axis=0)


def split2(m):
    hi = m.astype(jnp.bfloat16).astype(np.float32)
    lo = (m - hi).astype(np.float32)
    return hi, lo


def gauss_x(nx):
    w = np.array(blur_weights(), np.float32)
    d = np.arange(nx)[:, None] - np.arange(nx)[None, :]
    m = np.where(np.abs(d) <= GAUSS_R, w[np.clip(d + GAUSS_R, 0, 2 * GAUSS_R)], 0.0).astype(np.float32)
    hi, lo = split2(m)
    return np.concatenate([hi, hi, lo], axis=0)


def row_of(ny):
    nb = ny // 8
    r = np.arange(ny)
    i, s = r // 8, r % 8
    return s * nb + i


def gauss_y(ny, planes):
    w = np.array(blur_weights(), np.float32)
    y_in = row_of(ny)
    d = y_in[None, :] - np.arange(ny)[:, None]
    m = np.where(np.abs(d) <= GAUSS_R, w[np.clip(d + GAUSS_R, 0, 2 * GAUSS_R)], 0.0).astype(np.float32)
    m = np.kron(np.eye(planes, dtype=np.float32), m)
    hi, lo = split2(m)
    return np.concatenate([hi, hi, lo], axis=1)


def suffix_prefix(first, second):
    n = len(first)
    suf = [None] * n
    suf[n - 1] = first[n - 1]
    for i in range(n - 2, -1, -1):
        suf[i] = first[i] + suf[i + 1]
    out = []
    run = None
    for i in range(n):
        run = second[i] if run is None else run + second[i]
        out.append(suf[i] + run)
    return out


PEERS = ((0, 0), (1, 2), (0, 2), (1, 1), (1, 3), (0, 1), (0, 3), (1, 0))


def peer(s, dz, dy):
    return (s & 4) ^ (4 * dz) | ((s + dy) & 3)


def pack_kernel(me, src, full, head, tail, *rest):
    pieces, stage = rest[:-1], rest[-1]
    k = pl.program_id(0)
    idx = [peer(me[0], dz, dy) for dz, dy in PEERS]

    def natural(p, c):
        for h in range(2):
            stage[p, h] = src[p, :, pl.ds(128 * h, 128)]
        return c

    lax.fori_loop(0, BZ, natural, 0)

    def body(p, c):
        for h in range(2):
            for i in range(8):
                full[p, pl.ds(8 * i, 8), pl.ds(128 * h, 128)] = stage[p, h, pl.ds(i, 8, stride=8), :]
            for j, ref in enumerate(pieces):
                ref[p, :, pl.ds(128 * h, 128)] = stage[p, h, pl.ds(idx[j], 8, stride=8), :]
        return c

    lax.fori_loop(0, BZ, body, 0)

    @pl.when(k == 0)
    def _():
        head[...] = full[...]

    @pl.when(k == pl.num_programs(0) - 1)
    def _():
        tail[...] = full[...]


def pack_call(me, moving):
    planes = moving.shape[0]
    n = planes // BZ
    plane = moving.shape[1:]
    members = len(PEERS)
    block = jax.ShapeDtypeStruct((BZ,) + plane, F32)
    return pl.pallas_call(
        pack_kernel,
        name="pack",
        grid=(n,),
        in_specs=[pl.BlockSpec(memory_space=pltpu.SMEM), blk(lambda k: (k, 0, 0))],
        out_specs=[blk(lambda k: (k, 0, 0)), whole(block.shape), whole(block.shape)]
        + [pl.BlockSpec((BZ, 8, 256), lambda k: (k, 0, 0))] * members,
        out_shape=[jax.ShapeDtypeStruct(moving.shape, F32), block, block]
        + [jax.ShapeDtypeStruct((planes, 8, 256), F32)] * members,
        scratch_shapes=[pltpu.VMEM((BZ, 2, 64, 128), F32)],
        compiler_params=params(),
    )(me, moving)


def gather_kernel(me, *refs):
    n = len(PEERS)
    pieces, (full, head, tail) = refs[:n], refs[n:]
    k = pl.program_id(0)
    for piece, (dz, dy) in zip(pieces, PEERS):
        full[:, pl.ds(pl.multiple_of(peer(me[0], dz, dy) * 8, 8), 8), :] = piece[...]

    @pl.when(k == 0)
    def _():
        head[...] = full[...]

    @pl.when(k == pl.num_programs(0) - 1)
    def _():
        tail[...] = full[...]


def gather_call(me, pieces):
    n = len(pieces)
    planes, _, nx = pieces[0].shape
    block = jax.ShapeDtypeStruct((BZ, 8 * n, nx), F32)
    return pl.pallas_call(
        gather_kernel,
        name="gather",
        grid=(planes // BZ,),
        in_specs=[pl.BlockSpec(memory_space=pltpu.SMEM)] + [pl.BlockSpec((BZ, 8, nx), lambda k: (k, 0, 0))] * n,
        out_specs=[blk(lambda k: (k, 0, 0)), whole(block.shape), whole(block.shape)],
        out_shape=[jax.ShapeDtypeStruct((planes, 8 * n, nx), F32), block, block],
        compiler_params=params(),
    )(me, *pieces)


def natural_kernel(src, dst, stage):
    def rows(p, c):
        for h in range(2):
            stage[p, h] = src[p, :, pl.ds(128 * h, 128)]
        return c

    lax.fori_loop(0, BZ, rows, 0)

    def body(p, c):
        for h in range(2):
            for i in range(8):
                dst[p, pl.ds(8 * i, 8), pl.ds(128 * h, 128)] = stage[p, h, pl.ds(i, 8, stride=8), :]
        return c

    lax.fori_loop(0, BZ, body, 0)


def natural_call(array):
    return pl.pallas_call(
        natural_kernel,
        name="natural",
        grid=(array.shape[0] // BZ,),
        in_specs=[blk(lambda k: (k, 0, 0))],
        out_specs=blk(lambda k: (k, 0, 0)),
        out_shape=jax.ShapeDtypeStruct(array.shape, F32),
        scratch_shapes=[pltpu.VMEM((BZ, 2, 64, 128), F32)],
        compiler_params=params(),
    )(array)


def z_sums(out, terms, get_first, get_second):
    def body(q, c):
        rows = pl.ds(pl.multiple_of(q * 8, 8), 8)
        for h in range(2):
            cols = pl.ds(128 * h, 128)
            first = get_first(rows, cols)
            second = get_second(rows, cols)
            for ref, term in zip(out, terms):
                res = suffix_prefix([term(a) for a in first], [term(b) for b in second])
                for p in range(8):
                    ref[p, rows, cols] = res[p]
        return c

    lax.fori_loop(0, 8, body, 0)


def y_sums_split(ref, parts):
    sub = lax.broadcasted_iota(jnp.int32, (8, 128), 0)
    first_row, last_row = sub == 0, sub == 7

    def body(p, c):
        for h in range(2):
            cols = pl.ds(128 * h, 128)
            x = [ref[p, pl.ds(8 * i, 8), cols] for i in range(8)]
            down = [jnp.where(first_row, 0.0, pltpu.roll(x[i], 1, 0)) for i in range(4, 8)]
            up = [jnp.where(last_row, 0.0, pltpu.roll(x[i], 7, 0)) for i in range(4)]
            res = suffix_prefix(down + x[:4], x[4:] + up)
            for j in range(4):
                v = jnp.concatenate([res[2 * j], res[2 * j + 1]], axis=0)
                hi = v.astype(BF16)
                v = v - hi.astype(F32)
                mid = v.astype(BF16)
                lo = (v - mid.astype(F32)).astype(BF16)
                rows = pl.ds(pl.multiple_of(p * 64, 64) + 16 * j, 16)
                parts[rows, pl.ds(128 * h, 128)] = hi
                parts[rows, pl.ds(256 + 128 * h, 128)] = mid
                parts[rows, pl.ds(512 + 128 * h, 128)] = lo
        return c

    lax.fori_loop(0, 8, body, 0)


def x_sums(parts, band, out):
    out[...] = jnp.dot(parts[...], band[...], preferred_element_type=F32).reshape(out.shape)


def fetch_block(k, last, ring, slot, lo, body, hi):
    @pl.when(k == 0)
    def _():
        ring[slot] = lo[...]

    @pl.when(jnp.logical_and(k > 0, k < last))
    def _():
        ring[slot] = body[...]

    @pl.when(k == last)
    def _():
        ring[slot] = hi[...]


def moving_kernel(lo, body, hi, band, ip, mean, var, ring, zs, parts, sums):
    k = pl.program_id(0)
    last = pl.num_programs(0) - 1
    slot = lax.rem(k, 2)
    prev = 1 - slot
    fetch_block(k, last, ring, slot, lo, body, hi)
    ip[...] = ring[slot]

    @pl.when(k > 0)
    def _():
        z_sums(
            [zs.at[0], zs.at[1]],
            [lambda a: a, lambda a: a * a],
            lambda r, c: [ring[prev, p, r, c] for p in range(8)],
            lambda r, c: [ring[slot, p, r, c] for p in range(8)],
        )
        for v in range(2):
            y_sums_split(zs.at[v], parts)
            x_sums(parts, band, sums.at[v])

        def point(p, c):
            m = sums[0, p] * INV
            mean[p] = m
            var[p] = sums[1, p] * INV - m * m
            return c

        lax.fori_loop(0, 8, point, 0)


def blk(f):
    return pl.BlockSpec((BZ, 64, 256), f)


def whole(shape):
    return pl.BlockSpec(shape, lambda k: (0,) * len(shape))


def params(**kw):
    return pltpu.CompilerParams(vmem_limit_bytes=60 * 1024 * 1024, **kw)


def moving_call(moving, lo, hi):
    n = moving.shape[0] // BZ
    plane = moving.shape[1:]
    band = jnp.asarray(band_ones(256), BF16)
    clip = lambda k: jnp.clip(k - 1, 0, n - 1)
    return pl.pallas_call(
        moving_kernel,
        name="moving",
        grid=(n + 2,),
        in_specs=[whole(lo.shape), blk(lambda k: (clip(k), 0, 0)), whole(hi.shape), whole(band.shape)],
        out_specs=[blk(lambda k: (k, 0, 0)), blk(lambda k: (jnp.maximum(k - 1, 0), 0, 0)), blk(lambda k: (jnp.maximum(k - 1, 0), 0, 0))],
        out_shape=[jax.ShapeDtypeStruct(((n + 2) * BZ,) + plane, F32)] + [jax.ShapeDtypeStruct(((n + 1) * BZ,) + plane, F32)] * 2,
        scratch_shapes=[
            pltpu.VMEM((2, BZ, 64, 256), F32),
            pltpu.VMEM((2, BZ, 64, 256), F32),
            pltpu.VMEM((BZ * 64, 768), BF16),
            pltpu.VMEM((2, BZ, 64, 256), F32),
        ],
        compiler_params=params(),
    )(lo, moving, hi, band)


def factor_kernel(edge, lo, body, hi, ia, ib, mean, var, band, fac, total, ring, zs, parts, sums, loss):
    k = pl.program_id(0)
    last = pl.num_programs(0) - 1
    slot = lax.rem(k, 2)
    prev = 1 - slot
    fetch_block(k, last, ring, slot, lo, body, hi)

    @pl.when(k == 0)
    def _():
        loss[...] = jnp.zeros(loss.shape, F32)

    @pl.when(k > 0)
    def _():
        z_sums(
            [zs.at[0], zs.at[1]],
            [lambda a: a, lambda a: a * a],
            lambda r, c: [ring[prev, p, r, c] for p in range(8)],
            lambda r, c: [ring[slot, p, r, c] for p in range(8)],
        )
        z_sums(
            [zs.at[2]],
            [lambda a: a[0] * a[1]],
            lambda r, c: [(ring[prev, p, r, c], ia[p, r, c]) for p in range(8)],
            lambda r, c: [(ring[slot, p, r, c], ib[p, r, c]) for p in range(8)],
        )
        for v in range(3):
            y_sums_split(zs.at[v], parts)
            x_sums(parts, band, sums.at[v])

        def point(t, c):
            p = t >> 2
            rows = pl.ds(pl.multiple_of(lax.rem(t, 4) * 16, 16), 16)
            plane = (k - 1) * BZ - 4 + p
            inside = jnp.logical_and(plane >= 0, plane < (last - 1) * BZ)
            keep = jnp.logical_or(inside, jnp.where(plane < 0, edge[0], edge[1]) == 0)
            src_slot = jnp.where(p < 4, prev, slot)
            q = jnp.where(p < 4, p + 4, p - 4)
            j0 = ring[src_slot, q, rows, :]
            i0 = jnp.where(p < 4, ia[q, rows, :], ib[q, rows, :])
            mj = sums[0, p, rows, :] * INV
            vj = sums[1, p, rows, :] * INV - mj * mj
            mi = mean[p, rows, :]
            vi = var[p, rows, :]
            cc = sums[2, p, rows, :] * INV - mi * mj
            d1 = vi * vj + epsilon
            e = cc / d1
            sim = cc * e
            f = e * ((j0 - mj) - cc / (vi + epsilon) * (i0 - mi))
            fac[p, rows, :] = jnp.where(keep, f, 0.0)
            loss[...] += jnp.where(inside, sim, 0.0)
            return c

        lax.fori_loop(0, 32, point, 0)

    @pl.when(k == last)
    def _():
        total[0] = jnp.sum(loss[...])


def factor_call(edge, template, lo, hi, ip, mean, var):
    n = template.shape[0] // BZ
    plane = template.shape[1:]
    band = jnp.asarray(band_ones(256), BF16)
    clip = lambda k: jnp.clip(k - 1, 0, n - 1)
    back = lambda k: jnp.maximum(k - 1, 0)
    return pl.pallas_call(
        factor_kernel,
        name="factor",
        grid=(n + 2,),
        in_specs=[
            pl.BlockSpec(memory_space=pltpu.SMEM),
            whole(lo.shape), blk(lambda k: (clip(k), 0, 0)), whole(hi.shape),
            blk(lambda k: (back(k), 0, 0)), blk(lambda k: (jnp.maximum(k, 1), 0, 0)),
            blk(lambda k: (back(k), 0, 0)), blk(lambda k: (back(k), 0, 0)),
            whole(band.shape),
        ],
        out_specs=[blk(lambda k: (back(k), 0, 0)), pl.BlockSpec(memory_space=pltpu.SMEM)],
        out_shape=[jax.ShapeDtypeStruct(((n + 1) * BZ,) + plane, F32), jax.ShapeDtypeStruct((1,), F32)],
        scratch_shapes=[
            pltpu.VMEM((2, BZ, 64, 256), F32),
            pltpu.VMEM((3, BZ, 64, 256), F32),
            pltpu.VMEM((BZ * 64, 768), BF16),
            pltpu.VMEM((3, BZ, 64, 256), F32),
            pltpu.VMEM((16, 256), F32),
        ],
        compiler_params=params(),
    )(edge, lo, template, hi, ip, ip, mean, var, band)


def smooth_kernel(comp, fac, ia, ib, ax, ay, *rest):
    out, ring, xp, xs, yp = rest[-5:]
    k = pl.program_id(0)
    slot = lax.rem(k, 2)
    prev = 1 - slot
    sub = lax.broadcasted_iota(jnp.int32, (8, 128), 0)
    lane = lax.broadcasted_iota(jnp.int32, (8, 128), 1)

    def raw(p, mid, before, after):
        for i in range(8):
            rows = pl.ds(8 * i, 8)
            im = [mid(rows, pl.ds(128 * h, 128)) for h in range(2)]
            if comp == 2:
                left = [pltpu.roll(v, 127, 1) for v in im]
                right = [pltpu.roll(v, 1, 1) for v in im]
                e, s = lane == 127, lane == 0
                up = [jnp.where(e, left[1], left[0]), jnp.where(e, 0.0, left[1])]
                dn = [jnp.where(s, 0.0, right[0]), jnp.where(s, right[0], right[1])]
            for h in range(2):
                cols = pl.ds(128 * h, 128)
                if comp == 0:
                    slope = after(rows, cols) - before(rows, cols)
                elif comp == 1:
                    u = mid(pl.ds(8 * ((i + 1) % 8), 8), cols)
                    d = mid(pl.ds(8 * ((i + 7) % 8), 8), cols)
                    u = jnp.where(sub == 7, 0.0, pltpu.roll(u, 7, 0)) if i == 7 else u
                    d = jnp.where(sub == 0, 0.0, pltpu.roll(d, 1, 0)) if i == 0 else d
                    slope = u - d
                else:
                    slope = up[h] - dn[h]
                ring[slot, p, rows, cols] = fac[p, rows, cols] * slope

    def at(ref, q):
        return lambda r, c: ref[q, r, c]

    def lower(p, c):
        raw(p, at(ia, p + 4), at(ia, p + 3), at(ia, p + 5))
        return c

    def upper(p, c):
        raw(p, at(ib, p - 4), at(ib, p - 5), at(ib, p - 3))
        return c

    lax.fori_loop(0, 3, lower, 0)
    raw(3, at(ia, 7), at(ia, 6), at(ib, 0))
    raw(4, at(ib, 0), at(ia, 7), at(ib, 1))
    lax.fori_loop(5, 8, upper, 0)

    w = [float(v) for v in blur_weights()]

    @pl.when(k > 0)
    def _():
        def z_pass(q, c):
            rows = pl.ds(pl.multiple_of(q * 16, 16), 16)
            for h in range(2):
                cols = pl.ds(128 * h, 128)
                x = [ring[prev, p, rows, cols] for p in range(1, 8)] + [
                    ring[slot, p, rows, cols] for p in range(0, 7)]
                for p in range(8):
                    v = w[3] * x[p + 3]
                    for d in range(1, 4):
                        v = v + w[3 - d] * (x[p + 3 - d] + x[p + 3 + d])
                    hi = v.astype(BF16)
                    lo = (v - hi.astype(F32)).astype(BF16)
                    dst = pl.ds(64 * p + pl.multiple_of(q * 16, 16), 16)
                    xp[dst, pl.ds(128 * h, 128)] = hi
                    xp[dst, pl.ds(256 + 128 * h, 128)] = lo
                    xp[dst, pl.ds(512 + 128 * h, 128)] = hi
            return c

        lax.fori_loop(0, 4, z_pass, 0)
        xs[...] = jnp.dot(xp[...], ax[...], preferred_element_type=F32)

        def split(t, c):
            rows = pl.ds(pl.multiple_of(t * 32, 32), 32)
            v = xs[rows, :]
            hi = v.astype(BF16)
            g = t >> 3
            r = pl.multiple_of((t & 7) * 32, 32)
            yp[g, pl.ds(r, 32), :] = hi
            yp[g, pl.ds(256 + r, 32), :] = (v - hi.astype(F32)).astype(BF16)
            yp[g, pl.ds(512 + r, 32), :] = hi
            return c

        lax.fori_loop(0, 16, split, 0)
        for g in range(2):
            out[0, pl.ds(4 * g, 4)] = jnp.dot(
                ay[...], yp[g], preferred_element_type=F32).reshape(4, 64, 256)


def smooth_call(comp, fac, ip, force):
    n = fac.shape[0] // BZ - 1
    plane = fac.shape[1:]
    ax = jnp.asarray(gauss_x(256), BF16)
    ay = jnp.asarray(gauss_y(64, 4), BF16)
    kept = [] if force is None else [force]
    return pl.pallas_call(
        functools.partial(smooth_kernel, comp),
        name="smooth",
        grid=(n + 1,),
        in_specs=[blk(lambda k: (k, 0, 0)), blk(lambda k: (k, 0, 0)), blk(lambda k: (k + 1, 0, 0)),
                  whole(ax.shape), whole(ay.shape)] + [pl.BlockSpec(memory_space=pl.ANY)] * len(kept),
        out_specs=pl.BlockSpec((1, BZ, 64, 256), lambda k: (comp, jnp.maximum(k - 1, 0), 0, 0)),
        out_shape=jax.ShapeDtypeStruct((3, n * BZ) + plane, F32),
        input_output_aliases={5: 0} if kept else {},
        scratch_shapes=[
            pltpu.VMEM((2, BZ, 64, 256), F32),
            pltpu.VMEM((BZ * 64, 768), BF16),
            pltpu.VMEM((BZ * 64, 256), F32),
            pltpu.VMEM((2, 768, 256), BF16),
        ],
        compiler_params=params(),
    )(fac, ip, ip, ax, ay, *kept)


from jax.sharding import PartitionSpec as P


def shift(array, axis, step):
    size = lax.axis_size(axis)
    return lax.ppermute(array, axis, [(i, i + step) for i in range(size) if 0 <= i + step < size])


def steps(warped):
    moving = warped[0]
    planes = moving.shape[0]
    g, size = lax.axis_index("gz"), lax.axis_size("gz")
    edge = jnp.stack([g == 0, g == size - 1]).astype(jnp.int32)
    me = jnp.reshape(lax.axis_index("subj"), (1,)).astype(jnp.int32)
    pairs = [[(i, peer(i, dz, dy)) for i in range(8)] for dz, dy in PEERS]
    back = [[(b, a) for a, b in pair] for pair in pairs]

    full, head, tail, *pieces = pack_call(me, moving)
    got = [lax.ppermute(piece, "subj", pair) for piece, pair in zip(pieces[1:], pairs[1:])]
    lo, hi = shift(tail, "gz", 1), shift(head, "gz", -1)
    ip, mean, var = moving_call(full, lo, hi)
    got, mean, var = lax.optimization_barrier((got, mean, var))
    own = pieces[0]
    for piece in got:
        own = own + piece
    own = own * 0.125
    got = [own] + [lax.ppermute(own, "subj", pair) for pair in back[1:]]
    target, thead, ttail = gather_call(me, got)
    tlo, thi = shift(ttail, "gz", 1), shift(thead, "gz", -1)
    fac, total = factor_call(edge, target, tlo, thi, ip, mean, var)
    force = None
    for step, comp in zip((1, 2, 4, 8), (0, 1, 2, None)):
        other = lax.ppermute(total, "gz", [(i, i ^ step) for i in range(size)])
        if comp is not None:
            force = smooth_call(comp, fac, ip, force)
        total = total + other
    cells = float(size * planes * moving.shape[1] * moving.shape[2])
    return force[None], natural_call(target), -total / cells


def solution(mesh):
    return jax.shard_map(
        steps,
        mesh=mesh,
        in_specs=(P("subj", "gz", None, None),),
        out_specs=(P("subj", None, "gz", None, None), P("gz", None, None), P("subj")),
        check_vma=False,
    )
```

```python
import functools, math
import numpy as np
import jax
import jax.numpy as jnp
from jax import lax
from jax.experimental import pallas as pl
from jax.experimental.pallas import tpu as pltpu

BOX_R = 4
GAUSS_R = 3
epsilon = 1e-05
F32, BF16 = jnp.float32, jnp.bfloat16
BZ = 8
INV = 1.0 / 729.0


def blur_weights():
    bumps = [math.exp(-(k * k) / 8.0) for k in range(-GAUSS_R, GAUSS_R + 1)]
    whole = sum(bumps)
    return [b / whole for b in bumps]


def band_ones(nx):
    d = np.abs(np.arange(nx)[:, None] - np.arange(nx)[None, :])
    b = (d <= BOX_R).astype(np.float32)
    return np.concatenate([b, b, b], axis=0)


def split2(m):
    hi = m.astype(jnp.bfloat16).astype(np.float32)
    lo = (m - hi).astype(np.float32)
    return hi, lo


def gauss_x(nx):
    w = np.array(blur_weights(), np.float32)
    d = np.arange(nx)[:, None] - np.arange(nx)[None, :]
    m = np.where(np.abs(d) <= GAUSS_R, w[np.clip(d + GAUSS_R, 0, 2 * GAUSS_R)], 0.0).astype(np.float32)
    hi, lo = split2(m)
    return np.concatenate([hi, hi, lo], axis=0)


def row_of(ny):
    nb = ny // 8
    r = np.arange(ny)
    i, s = r // 8, r % 8
    return s * nb + i


def gauss_y(ny, planes):
    w = np.array(blur_weights(), np.float32)
    y_in = row_of(ny)
    d = y_in[None, :] - np.arange(ny)[:, None]
    m = np.where(np.abs(d) <= GAUSS_R, w[np.clip(d + GAUSS_R, 0, 2 * GAUSS_R)], 0.0).astype(np.float32)
    m = np.kron(np.eye(planes, dtype=np.float32), m)
    hi, lo = split2(m)
    return np.concatenate([hi, hi, lo], axis=1)


def suffix_prefix(first, second):
    n = len(first)
    suf = [None] * n
    suf[n - 1] = first[n - 1]
    for i in range(n - 2, -1, -1):
        suf[i] = first[i] + suf[i + 1]
    out = []
    run = None
    for i in range(n):
        run = second[i] if run is None else run + second[i]
        out.append(suf[i] + run)
    return out


PEERS = ((0, 0), (1, 2), (0, 2), (1, 1), (1, 3), (0, 1), (0, 3), (1, 0))
VM = pl.BlockSpec(memory_space=pltpu.VMEM)
SM = pl.BlockSpec(memory_space=pltpu.SMEM)
HB = pl.BlockSpec(memory_space=pltpu.HBM)


def peer(s, dz, dy):
    return (s & 4) ^ (4 * dz) | ((s + dy) & 3)


def params():
    return pltpu.CompilerParams(vmem_limit_bytes=20 * 1024 * 1024)


def volume(planes, rows=64):
    return jax.ShapeDtypeStruct((planes, rows, 256), F32)


def pack_kernel(me, src, full, head, tail, *rest):
    pieces, (stage, sem) = rest[:-2], rest[-2:]
    idx = [pl.multiple_of(peer(me[0], dz, dy) * 8, 8) for dz, dy in PEERS]
    n = src.shape[0] // BZ
    copies = [
        [
            pltpu.make_async_copy(
                src.at[pl.ds(BZ * b, BZ), :, pl.ds(128 * h, 128)], stage.at[h, pl.ds(BZ * b, BZ)], sem.at[b, h])
            for h in range(2)
        ]
        for b in range(n)
    ]
    for pair in copies:
        for copy in pair:
            copy.start()

    def body(p, c):
        for i in range(8):
            for h in range(2):
                full[p, pl.ds(8 * i, 8), pl.ds(128 * h, 128)] = stage[h, p, pl.ds(i, 8, stride=8), :]
        return c

    def cut(p, c):
        for ref, row in zip(pieces, idx):
            ref[p] = full[p, pl.ds(row, 8), :]
        return c
    for b in range(n):
        for copy in copies[b]:
            copy.wait()
        lax.fori_loop(BZ * b, BZ * (b + 1), body, 0)
        lax.fori_loop(BZ * b, BZ * (b + 1), cut, 0)
    head[...] = full[:BOX_R]
    tail[...] = full[BZ * n - BOX_R:]


def pack_call(me, moving):
    planes = moving.shape[0]
    return pl.pallas_call(
        pack_kernel,
        name="pack",
        in_specs=[SM, HB],
        out_specs=[VM] * (3 + len(PEERS)),
        out_shape=[volume(planes), volume(BOX_R), volume(BOX_R)] + [volume(planes, 8)] * len(PEERS),
        scratch_shapes=[pltpu.VMEM((2, planes, 64, 128), F32), pltpu.SemaphoreType.DMA((planes // BZ, 2))],
        compiler_params=params(),
    )(me, moving)


def gather_kernel(me, *refs):
    n = len(PEERS)
    pieces, (full, head, tail) = refs[:n], refs[n:]
    idx = [pl.multiple_of(peer(me[0], dz, dy) * 8, 8) for dz, dy in PEERS]

    def body(p, c):
        for piece, row in zip(pieces, idx):
            full[p, pl.ds(row, 8), :] = piece[p]
        return c
    planes = full.shape[0]
    lax.fori_loop(0, planes, body, 0)
    head[...] = full[:BOX_R]
    tail[...] = full[planes - BOX_R:]


def gather_call(me, pieces):
    planes = pieces[0].shape[0]
    return pl.pallas_call(
        gather_kernel,
        name="gather",
        in_specs=[SM] + [VM] * len(pieces),
        out_specs=[VM] * 3,
        out_shape=[volume(planes), volume(BOX_R), volume(BOX_R)],
        compiler_params=params(),
    )(me, *pieces)


def natural_kernel(src, dst, stage, out, sem):
    n = src.shape[0] // BZ

    def fill(p, c):
        for h in range(2):
            stage[p, h] = src[p, :, pl.ds(128 * h, 128)]
        return c

    def body(p, c):
        for h in range(2):
            for i in range(8):
                out[p, pl.ds(8 * i, 8), pl.ds(128 * h, 128)] = stage[p, h, pl.ds(i, 8, stride=8), :]
        return c
    copies = []
    for b in range(n):
        lax.fori_loop(BZ * b, BZ * (b + 1), fill, 0)
        lax.fori_loop(BZ * b, BZ * (b + 1), body, 0)
        block = pl.ds(BZ * b, BZ)
        copies.append(pltpu.make_async_copy(out.at[block], dst.at[block], sem.at[b]))
        copies[-1].start()
    for copy in copies:
        copy.wait()


def natural_call(array):
    planes = array.shape[0]
    return pl.pallas_call(
        natural_kernel,
        name="natural",
        in_specs=[VM],
        out_specs=HB,
        out_shape=volume(planes),
        scratch_shapes=[
            pltpu.VMEM((planes, 2, 64, 128), F32),
            pltpu.VMEM((planes, 64, 256), F32),
            pltpu.SemaphoreType.DMA((planes // BZ,)),
        ],
        compiler_params=params(),
    )(array)


def edge_sums(items):
    core = items[3]
    for v in items[4:9]:
        core = core + v
    s2, p9 = items[2], items[9]
    s1 = items[1] + s2
    p10 = p9 + items[10]
    return [items[0] + s1 + core, s1 + core + p9, s2 + core + p10, core + (p10 + items[11])]


def z_loop(out, terms, get):
    def body(q, c):
        rows = pl.ds(pl.multiple_of(q * 8, 8), 8)
        for h in range(2):
            cols = pl.ds(128 * h, 128)
            one, two = get(rows, cols)
            for ref, term in zip(out, terms):
                a, b = [term(v) for v in one], [term(v) for v in two]
                res = suffix_prefix(a, b) if len(a) == 8 else edge_sums(a) + edge_sums(b)
                for p in range(8):
                    ref[p, rows, cols] = res[p]
        return c
    lax.fori_loop(0, 8, body, 0)


def y_sums_split(ref, parts):
    sub = lax.broadcasted_iota(jnp.int32, (8, 128), 0)
    first_row, last_row = sub == 0, sub == 7

    def body(p, c):
        for h in range(2):
            cols = pl.ds(128 * h, 128)
            x = [ref[p, pl.ds(8 * i, 8), cols] for i in range(8)]
            down = [jnp.where(first_row, 0.0, pltpu.roll(x[i], 1, 0)) for i in range(4, 8)]
            up = [jnp.where(last_row, 0.0, pltpu.roll(x[i], 7, 0)) for i in range(4)]
            res = suffix_prefix(down + x[:4], x[4:] + up)
            for j in range(4):
                v = jnp.concatenate([res[2 * j], res[2 * j + 1]], axis=0)
                hi = v.astype(BF16)
                v = v - hi.astype(F32)
                mid = v.astype(BF16)
                lo = (v - mid.astype(F32)).astype(BF16)
                rows = pl.ds(pl.multiple_of(p * 64, 64) + 16 * j, 16)
                parts[rows, pl.ds(128 * h, 128)] = hi
                parts[rows, pl.ds(256 + 128 * h, 128)] = mid
                parts[rows, pl.ds(512 + 128 * h, 128)] = lo
        return c
    lax.fori_loop(0, 8, body, 0)


def x_sums(parts, band, out):
    out[...] = jnp.dot(parts[...], band[...], preferred_element_type=F32).reshape(out.shape)


def mid_planes(ref, j):
    return lambda r, c: ([ref[8 * j + p, r, c] for p in range(8)], [ref[8 * j + 8 + p, r, c] for p in range(8)])


def edge_planes(lo, ref, hi):
    n = ref.shape[0]
    return lambda r, c: (
        [lo[p, r, c] for p in range(4)] + [ref[p, r, c] for p in range(8)],
        [ref[n - 8 + p, r, c] for p in range(8)] + [hi[p, r, c] for p in range(4)],
    )


def both(get_a, get_b):
    def get(r, c):
        a, b = get_a(r, c), get_b(r, c)
        return tuple(list(zip(x, y)) for x, y in zip(a, b))
    return get


def moving_block(get, band, mean, var, at, zs, parts, sums):
    z_loop([zs.at[0], zs.at[1]], [lambda a: a, lambda a: a * a], get)
    for v in range(2):
        y_sums_split(zs.at[v], parts)
        x_sums(parts, band, sums.at[v])

    def point(p, c):
        m = sums[0, p] * INV
        mean[at + p] = m
        var[at + p] = sums[1, p] * INV - m * m
        return c
    lax.fori_loop(0, 8, point, 0)


def moving_mid_kernel(ip, band, mean, var, zs, parts, sums):
    def step(j, c):
        moving_block(mid_planes(ip, j), band, mean, var, 8 * j, zs, parts, sums)
        return c
    lax.fori_loop(0, mean.shape[0] // BZ, step, 0)


def moving_edge_kernel(lo, ip, hi, band, mean, var, zs, parts, sums):
    moving_block(edge_planes(lo, ip, hi), band, mean, var, 0, zs, parts, sums)


def box_scratch(v):
    return [
        pltpu.VMEM((v, BZ, 64, 256), F32),
        pltpu.VMEM((BZ * 64, 768), BF16),
        pltpu.VMEM((v, BZ, 64, 256), F32),
    ]


def moving_call(*images):
    planes = images[0].shape[0] - BZ if len(images) == 1 else BZ
    return pl.pallas_call(
        moving_mid_kernel if len(images) == 1 else moving_edge_kernel,
        name="moving",
        in_specs=[VM] * (len(images) + 1),
        out_specs=[VM] * 2,
        out_shape=[volume(planes)] * 2,
        scratch_shapes=box_scratch(2),
        compiler_params=params(),
    )(*images, jnp.asarray(band_ones(256), BF16))


def factor_block(get_t, get_i, cell_t, cell_i, mean, var, at, band, fac, loss, zs, parts, sums):
    z_loop([zs.at[0], zs.at[1]], [lambda a: a, lambda a: a * a], get_t)
    z_loop([zs.at[2]], [lambda a: a[0] * a[1]], both(get_t, get_i))
    for v in range(3):
        y_sums_split(zs.at[v], parts)
        x_sums(parts, band, sums.at[v])

    def point(t, c):
        p = t >> 2
        rows = pl.ds(pl.multiple_of((t & 3) * 16, 16), 16)
        j0 = cell_t(p, rows)
        i0 = cell_i(p, rows)
        mj = sums[0, p, rows, :] * INV
        vj = sums[1, p, rows, :] * INV - mj * mj
        mi = mean[at + p, rows, :]
        vi = var[at + p, rows, :]
        cc = sums[2, p, rows, :] * INV - mi * mj
        e = cc / (vi * vj + epsilon)
        fac[at + p, rows, :] = e * ((j0 - mj) - cc / (vi + epsilon) * (i0 - mi))
        loss[...] += cc * e
        return c
    lax.fori_loop(0, 32, point, 0)


def factor_mid_kernel(t, ip, mean, var, band, fac, total, zs, parts, sums, loss):
    loss[...] = jnp.zeros(loss.shape, F32)

    def step(j, c):
        cell = lambda ref: lambda p, rows: ref[8 * j + 4 + p, rows, :]
        factor_block(mid_planes(t, j), mid_planes(ip, j), cell(t), cell(ip), mean, var, 8 * j, band, fac, loss,
                     zs, parts, sums)
        return c
    lax.fori_loop(0, fac.shape[0] // BZ, step, 0)
    total[0] = jnp.sum(loss[...])


def factor_edge_kernel(tlo, t, thi, ilo, ip, ihi, mean, var, before, band, fac, first, last, total, zs, parts, sums, loss):
    loss[...] = jnp.zeros(loss.shape, F32)
    n = t.shape[0]
    cell = lambda ref: lambda p, rows: ref[jnp.where(p < 4, p, n - 8 + p), rows, :]
    factor_block(edge_planes(tlo, t, thi), edge_planes(ilo, ip, ihi), cell(t), cell(ip), mean, var, 0, band, fac, loss,
                 zs, parts, sums)
    first[...] = fac[:GAUSS_R]
    last[...] = fac[BZ - GAUSS_R:]
    total[0] = before[0] + jnp.sum(loss[...])


def factor_mid_call(target, full, mean, var):
    return pl.pallas_call(
        factor_mid_kernel,
        name="factor",
        in_specs=[VM] * 5,
        out_specs=[VM, SM],
        out_shape=[volume(mean.shape[0]), jax.ShapeDtypeStruct((1,), F32)],
        scratch_shapes=box_scratch(3) + [pltpu.VMEM((16, 256), F32)],
        compiler_params=params(),
    )(target, full, mean, var, jnp.asarray(band_ones(256), BF16))


def factor_edge_call(tlo, target, thi, ilo, full, ihi, mean, var, total):
    return pl.pallas_call(
        factor_edge_kernel,
        name="factor_edge",
        in_specs=[VM] * 8 + [SM, VM],
        out_specs=[VM] * 3 + [SM],
        out_shape=[volume(BZ), volume(GAUSS_R), volume(GAUSS_R), jax.ShapeDtypeStruct((1,), F32)],
        scratch_shapes=box_scratch(3) + [pltpu.VMEM((16, 256), F32)],
        compiler_params=params(),
    )(tlo, target, thi, ilo, full, ihi, mean, var, total, jnp.asarray(band_ones(256), BF16))


def raw_planes(comp, n, fac_at, image_at, raw):
    sub = lax.broadcasted_iota(jnp.int32, (8, 128), 0)
    lane = lax.broadcasted_iota(jnp.int32, (8, 128), 1)

    def body(q, c):
        mid = image_at(q)
        for i in range(8):
            rows = pl.ds(8 * i, 8)
            if comp == 2:
                im = [mid(rows, pl.ds(128 * h, 128)) for h in range(2)]
                left = [pltpu.roll(v, 127, 1) for v in im]
                right = [pltpu.roll(v, 1, 1) for v in im]
                e, s = lane == 127, lane == 0
                up = [jnp.where(e, left[1], left[0]), jnp.where(e, 0.0, left[1])]
                dn = [jnp.where(s, 0.0, right[0]), jnp.where(s, right[0], right[1])]
            for h in range(2):
                cols = pl.ds(128 * h, 128)
                if comp == 0:
                    slope = image_at(q + 1)(rows, cols) - image_at(q - 1)(rows, cols)
                elif comp == 1:
                    u = mid(pl.ds(8 * ((i + 1) % 8), 8), cols)
                    d = mid(pl.ds(8 * ((i + 7) % 8), 8), cols)
                    u = jnp.where(sub == 7, 0.0, pltpu.roll(u, 7, 0)) if i == 7 else u
                    d = jnp.where(sub == 0, 0.0, pltpu.roll(d, 1, 0)) if i == 0 else d
                    slope = u - d
                else:
                    slope = up[h] - dn[h]
                raw[q, rows, cols] = fac_at(q)(rows, cols) * slope
        return c
    lax.fori_loop(0, n, body, 0)


def blur_block(raw, at, ax, ay, out, xp, xs, yp):
    w = [float(v) for v in blur_weights()]

    def z_pass(q, c):
        top = pl.multiple_of(q * 16, 16)
        rows = pl.ds(top, 16)
        for h in range(2):
            cols = pl.ds(128 * h, 128)
            x = [raw[at + p, rows, cols] for p in range(14)]
            for p in range(8):
                v = w[3] * x[p + 3]
                for d in range(1, 4):
                    v = v + w[3 - d] * (x[p + 3 - d] + x[p + 3 + d])
                hi = v.astype(BF16)
                lo = (v - hi.astype(F32)).astype(BF16)
                dst = pl.ds(64 * p + top, 16)
                xp[dst, pl.ds(128 * h, 128)] = hi
                xp[dst, pl.ds(256 + 128 * h, 128)] = lo
                xp[dst, pl.ds(512 + 128 * h, 128)] = hi
        return c
    lax.fori_loop(0, 4, z_pass, 0)
    xs[...] = jnp.dot(xp[...], ax[...], preferred_element_type=F32)

    def split(t, c):
        rows = pl.ds(pl.multiple_of(t * 32, 32), 32)
        v = xs[rows, :]
        hi = v.astype(BF16)
        g = t >> 3
        r = pl.multiple_of((t & 7) * 32, 32)
        yp[g, pl.ds(r, 32), :] = hi
        yp[g, pl.ds(256 + r, 32), :] = (v - hi.astype(F32)).astype(BF16)
        yp[g, pl.ds(512 + r, 32), :] = hi
        return c
    lax.fori_loop(0, 16, split, 0)
    for g in range(2):
        out[pl.ds(4 * g, 4)] = jnp.dot(ay[...], yp[g], preferred_element_type=F32).reshape(4, 64, 256)


def at_plane(ref):
    return lambda q: lambda r, c: ref[q, r, c]


def blur_mid_kernel(comp, fac, ip, ax, ay, *rest):
    force, raw, out, xp, xs, yp, sem = rest[-7:]
    n = fac.shape[0]
    raw_planes(comp, n, at_plane(fac), lambda q: at_plane(ip)(q + 4), raw)
    copies = []
    for m in range(n // BZ - 1):
        blur_block(raw, BZ * m + 1, ax, ay, out.at[m], xp, xs, yp)
        copies.append(pltpu.make_async_copy(out.at[m], force.at[comp, pl.ds(BZ * (m + 1), BZ)], sem.at[m]))
        copies[-1].start()
    for copy in copies:
        copy.wait()


def blur_edge_kernel(facm, face, flo, fhi, ilo, ip, ihi, ax, ay, before, force, image, fac, raw, out, xp, xs, yp, sem):
    n = ip.shape[0]
    m = facm.shape[0]
    copies = []
    for side in range(2):
        if side == 0:
            image[:4] = ilo[...]
            image[4:20] = ip[:16]
            fac[:3] = flo[...]
            fac[3:7] = face[:4]
            fac[7:14] = facm[:7]
        else:
            image[:16] = ip[n - 16:]
            image[16:20] = ihi[...]
            fac[:7] = facm[m - 7:]
            fac[7:11] = face[4:]
            fac[11:14] = fhi[...]
        shift = 1 if side == 0 else 5
        for comp in range(3):
            raw_planes(comp, 14, at_plane(fac), lambda q: at_plane(image)(q + shift), raw)
            slot = 3 * side + comp
            blur_block(raw, 0, ax, ay, out.at[slot], xp, xs, yp)
            copies.append(pltpu.make_async_copy(
                out.at[slot], force.at[comp, pl.ds(0 if side == 0 else n - BZ, BZ)], sem.at[slot]))
            copies[-1].start()
    for copy in copies:
        copy.wait()


def blur_scratch(planes, blocks):
    return [
        pltpu.VMEM((planes, 64, 256), F32),
        pltpu.VMEM((blocks, BZ, 64, 256), F32),
        pltpu.VMEM((BZ * 64, 768), BF16),
        pltpu.VMEM((BZ * 64, 256), F32),
        pltpu.VMEM((2, 768, 256), BF16),
        pltpu.SemaphoreType.DMA((blocks,)),
    ]


def blur_mid_call(comp, fac, full, force):
    n = fac.shape[0]
    kept = [] if force is None else [force]
    return pl.pallas_call(
        functools.partial(blur_mid_kernel, comp),
        name="blur",
        in_specs=[VM] * 4 + [HB] * len(kept),
        out_specs=HB,
        out_shape=jax.ShapeDtypeStruct((3,) + full.shape, F32),
        input_output_aliases={4: 0} if kept else {},
        scratch_shapes=blur_scratch(n, n // BZ - 1),
        compiler_params=params(),
    )(fac, full, jnp.asarray(gauss_x(256), BF16), jnp.asarray(gauss_y(64, 4), BF16), *kept)


def blur_edge_call(facm, face, flo, fhi, ilo, full, ihi, force):
    return pl.pallas_call(
        blur_edge_kernel,
        name="blur_edge",
        in_specs=[VM] * 9 + [HB],
        out_specs=HB,
        out_shape=jax.ShapeDtypeStruct((3,) + full.shape, F32),
        input_output_aliases={9: 0},
        scratch_shapes=[pltpu.VMEM((20, 64, 256), F32), pltpu.VMEM((14, 64, 256), F32)] + blur_scratch(14, 6),
        compiler_params=params(),
    )(facm, face, flo, fhi, ilo, full, ihi, jnp.asarray(gauss_x(256), BF16), jnp.asarray(gauss_y(64, 4), BF16), force)


from jax.sharding import PartitionSpec as P


def halo(first, last, size):
    up = [(i, i + 1) for i in range(size - 1)]
    down = [(j, i) for i, j in up]
    return lax.ppermute(last, "gz", up), lax.ppermute(first, "gz", down)


def steps(warped):
    moving = warped[0]
    planes = moving.shape[0]
    size = lax.axis_size("gz")
    me = jnp.reshape(lax.axis_index("subj"), (1,)).astype(jnp.int32)
    pairs = [[(i, peer(i, dz, dy)) for i in range(8)] for dz, dy in PEERS]
    back = [[(b, a) for a, b in pair] for pair in pairs]

    full, head, tail, *pieces = pack_call(me, moving)
    got = [lax.ppermute(pieces[j], "subj", pairs[j]) for j in range(1, 8)]
    ilo, ihi = halo(head, tail, size)
    mean, var = moving_call(full)
    own = pieces[0]
    for piece in got:
        own = own + piece
    own = own * 0.125
    got = [own] + [lax.ppermute(own, "subj", back[j]) for j in range(1, 8)]
    mean_e, var_e = moving_call(ilo, full, ihi)
    target, thead, ttail = gather_call(me, got)
    tlo, thi = halo(thead, ttail, size)
    fac, total = factor_mid_call(target, full, mean, var)
    fac_e, first, last, total = factor_edge_call(tlo, target, thi, ilo, full, ihi, mean_e, var_e, total)
    flo, fhi = halo(first, last, size)
    force = None
    for n, step in enumerate((1, 2, 4, 8)):
        other = lax.ppermute(total, "gz", [(i, i ^ step) for i in range(size)])
        if n < 3:
            force = blur_mid_call(n, fac, full, force)
        else:
            force = blur_edge_call(fac, fac_e, flo, fhi, ilo, full, ihi, force)
        total = total + other
    cells = float(size * planes * moving.shape[1] * moving.shape[2])
    template = natural_call(target)
    return force[None], template, -total / cells


def solution(mesh):
    return jax.shard_map(
        steps,
        mesh=mesh,
        in_specs=(P("subj", "gz", None, None),),
        out_specs=(P("subj", None, "gz", None, None), P("gz", None, None), P("subj")),
        check_vma=False,
    )
```
